768 devices in a mesh: expert: 96 (over z, y), etp: 8 (over x, core).
Axes of the slice: x: 4, y: 8, z: 12, core: 2. Of those that a mesh axis runs over, the one named last changes fastest.
Arguments:
- hidden_in: bfloat16 [1152, 4096], P('expert', 'etp'), may hold values from -6 to 6
- expert_ids: int32 [1152, 8], P('expert'), may hold values from 0 to 95, all different within a row; in each aligned block of 12 rows (0 to 11, 12 to 23, ...) at most 2 rows name the same one
- gate_weights: float32 [1152, 8], P('expert'), may hold values from 0.2 to 1
- out_grad: bfloat16 [1152, 4096], P('expert', 'etp'), may hold values from -6 to 6
- gate_weight: bfloat16 [96, 4096, 1024], P('expert', None, 'etp'), may hold values from -0.09375 to 0.09375
- up_weight: bfloat16 [96, 4096, 1024], P('expert', None, 'etp'), may hold values from -0.09375 to 0.09375
- down_weight: bfloat16 [96, 1024, 4096], P('expert', 'etp'), may hold values from -0.1875 to 0.1875
Outputs:
- mixed_out: bfloat16 [1152, 4096], P('expert', 'etp')
- input_grad: bfloat16 [1152, 4096], P('expert', 'etp')
- down_grad: bfloat16 [96, 1024, 4096], P('expert', 'etp')
The draws below stay inside these ranges and needn't reach their ends.
Inputs may be any that keep to these rules, and one draw needn't show every extreme that they name: `expert_ids`: each token names 8 different experts. Within each aligned block of 12 tokens no expert is named by more than 2 tokens, and in some block an expert is named by exactly 2 tokens.
All inputs are finite; a program needn't handle non-finite values.
Results may differ from the reference program's by a relative error of at most 0.018.
Values may be sent and summed in bfloat16 or wider, within the bound.
A program may use at most 32 MiB of HBM per device.

```python
import math
import jax
import jax.numpy as jnp
import numpy as np
from jax import lax

D = 4096
TOP = 8
F = 1024
TOK = 12
EXPERTS = 96
TOKENS = 1152
CAP = 2
N_EXPERT = 96
N_ETP = 8


def block_levels(stream_key, extent, shards, low, top_value):
    def one(dim, blocks):
        draws = jax.random.uniform(jax.random.fold_in(jax.random.fold_in(stream_key, 6), dim), (blocks,), jnp.float32, low / len(shards), top_value / len(shards))
        return jnp.repeat(jnp.exp(draws), extent[dim] // blocks).reshape((-1,) + (1,) * (len(extent) - dim - 1))

    gain = one(*shards[0])
    for cut in shards[1:]:
        gain = gain * one(*cut)
    return gain


def assign_block(stream_key, own, number, rows, amount, top, limit, lean):
    ranking = jax.random.permutation(stream_key, amount)
    crowded, usual = portions_of(amount, rows * top, limit, lean, True), portions_of(amount, rows * top, limit, lean, False)
    places = jnp.arange(amount)

    def named(tallies, turn):
        used = int((tallies > 0).sum())
        fixed = max(1, used // 4)
        shifted = fixed + (places - fixed + turn * (used - fixed)) % max(1, amount - fixed)
        return jnp.zeros((amount,), jnp.int32).at[ranking[jnp.where(places < fixed, places, shifted)]].set(jnp.asarray(tallies, jnp.int32))

    tallies = jnp.where(number % 4 == 0, named(crowded, number // 4), named(usual, number - number // 4 - 1))
    mixed = jax.random.permutation(jax.random.fold_in(own, 3), amount)
    source_of, sink = mixed[0:amount // 2 * 2:2], mixed[1:amount // 2 * 2:2]
    margin = jnp.minimum(tallies[source_of] - 1, limit - tallies[sink]) // 2
    margin = jnp.where((source_of == ranking[0]) | (sink == ranking[0]) | (tallies[sink] == 0), 0, jnp.maximum(margin, 0))
    shifted = jax.random.randint(jax.random.fold_in(own, 4), (amount // 2,), 0, 1 << 20) % (margin + 1)
    tallies = tallies.at[source_of].add(-shifted).at[sink].add(shifted)
    items = jnp.searchsorted(jnp.cumsum(tallies), jnp.arange(rows * top), side="right").astype(jnp.int32)
    grid = items.reshape(top, rows).T
    grid = grid[jax.random.permutation(jax.random.fold_in(own, 1), rows)]
    turn = jax.random.randint(jax.random.fold_in(own, 2), (rows, 1), 0, top)
    return jnp.take_along_axis(grid, (jnp.arange(top)[None, :] + turn) % top, axis=1)


def portions_of(amount, total, bound, skew, full):
    loads = [(1 << 20) // math.isqrt(grade ** skew) + 1 for grade in range(1, amount + 1)]
    largest = bound if full else min(bound, max(-(-total // amount), total * loads[0] // sum(loads)))
    least = 1 if total - largest >= amount - 1 else 0
    holding, surplus = [largest] + [least] * (amount - 1), total - largest - least * (amount - 1)
    while surplus > 0:
        movable = [i for i in range(1, amount) if holding[i] < largest] or [i for i in range(1, amount) if holding[i] < bound]
        mass, left = sum([loads[i] for i in movable]), surplus
        for i in movable:
            extra = min(bound - holding[i], max(1, left * loads[i] // mass), surplus)
            holding[i] = holding[i] + extra
            surplus = surplus - extra
    return np.array(holding)


def gaussian(own_key, extent, scale, reach, shards=(), kind=jnp.bfloat16):
    entries = jax.random.normal(own_key, extent, jnp.float32) * scale
    if len(shards) > 0:
        entries = block_levels(own_key, extent, shards, -0.22, 0.18) * entries
    return jnp.clip(entries, min=-reach, max=reach).astype(kind)


def setup_inputs(seed: int = 0) -> dict:
    keys = jax.random.split(jax.random.key(seed), 8)
    hidden_in = gaussian(keys[0], (TOKENS, D), 1.0, 6.0, ((0, 96), (1, 8)))
    expert_ids_keys = jax.random.split(jax.random.fold_in(keys[1], 1), TOKENS // TOK)
    expert_ids_turns = jax.random.permutation(jax.random.fold_in(keys[1], 3), TOKENS // TOK)
    expert_ids = jax.vmap(lambda own, number: assign_block(jax.random.fold_in(keys[1], 2), own, number, TOK, EXPERTS, TOP, CAP, 2))(expert_ids_keys, expert_ids_turns).reshape((TOKENS, TOP))
    gate_weights = jnp.clip(0.2 + 0.8 * jax.random.uniform(keys[2], (TOKENS, TOP), jnp.float32) ** block_levels(keys[2], (TOKENS, TOP), ((0, 96),), -0.2, 0.2), 0.2, 1.0)
    out_grad = gaussian(keys[3], (TOKENS, D), 1.0, 6.0, ((0, 96), (1, 8)))
    gate_weight = gaussian(keys[4], (EXPERTS, D, F), D ** -0.5, 0.09375, ((0, 96), (2, 8)))
    up_weight = gaussian(keys[5], (EXPERTS, D, F), D ** -0.5, 0.09375, ((0, 96), (2, 8)))
    down_weight = gaussian(keys[6], (EXPERTS, F, D), F ** -0.5, 0.1875, ((0, 96), (1, 8)))
    return dict(hidden_in=hidden_in, expert_ids=expert_ids, gate_weights=gate_weights, out_grad=out_grad, gate_weight=gate_weight, up_weight=up_weight, down_weight=down_weight)


def group_terms(left, right):
    row_count = left.shape[0]
    width = right.shape[0]
    left_groups = left.astype(jnp.float32).reshape(row_count, N_ETP, F // N_ETP)
    right_groups = right.astype(jnp.float32).reshape(width, N_ETP, F // N_ETP)
    return jnp.einsum("rgf,dgf->grd", left_groups, right_groups, precision=lax.Precision.HIGHEST)


def summed_groups(terms):
    rounded = lax.optimization_barrier(terms.astype(jnp.bfloat16))
    return jnp.sum(rounded.astype(jnp.float32), axis=0).astype(jnp.bfloat16)


def reference(hidden_in, expert_ids, gate_weights, out_grad, gate_weight, up_weight, down_weight):
    row_count = N_EXPERT * CAP
    blocks = expert_ids.reshape(N_EXPERT, TOK * TOP)
    onehot = (blocks[:, :, None] == jnp.arange(EXPERTS, dtype=jnp.int32)[None, None, :]).astype(jnp.int32)
    slot_rank = jnp.sum((jnp.cumsum(onehot, axis=1) - onehot) * onehot, axis=2)
    source = jnp.arange(N_EXPERT, dtype=jnp.int32)[:, None]
    position = (blocks * row_count + source * CAP + slot_rank).reshape(-1).astype(jnp.int32)
    filler = jnp.arange(TOKENS * TOP, dtype=jnp.int32) + 1
    table = jnp.zeros((EXPERTS * row_count,), jnp.int32).at[position].set(filler)
    table = table.reshape(EXPERTS, row_count)
    gate_flat = gate_weights.reshape(-1)

    def one_expert(operands):
        entry_code, gate_matrix, up_matrix, down_matrix = operands
        is_live = entry_code > 0
        slot_index = jnp.maximum(entry_code - 1, 0)
        token_index = slot_index // TOP
        rows_in = jnp.where(is_live[:, None], hidden_in[token_index], jnp.zeros((), jnp.bfloat16))
        scaled = (out_grad[token_index].astype(jnp.float32) * gate_flat[slot_index][:, None]).astype(jnp.bfloat16)
        grad_in = jnp.where(is_live[:, None], scaled, jnp.zeros((), jnp.bfloat16))
        gate_pre = jnp.dot(rows_in, gate_matrix, preferred_element_type=jnp.float32)
        up_pre = jnp.dot(rows_in, up_matrix, preferred_element_type=jnp.float32)
        sigmoid_gate = jax.nn.sigmoid(gate_pre)
        swish_gate = gate_pre * sigmoid_gate
        hidden_act = (swish_gate * up_pre).astype(jnp.bfloat16)
        expert_out = summed_groups(group_terms(hidden_act, down_matrix.T))
        act_grad = jnp.dot(grad_in, down_matrix.T, preferred_element_type=jnp.float32)
        down_grad = jnp.dot(hidden_act.T, grad_in, preferred_element_type=jnp.float32).astype(jnp.bfloat16)
        gate_grad = (act_grad * up_pre * sigmoid_gate * (1.0 + gate_pre * (1.0 - sigmoid_gate))).astype(jnp.bfloat16)
        up_grad = (act_grad * swish_gate).astype(jnp.bfloat16)
        slot_dx = summed_groups(group_terms(gate_grad, gate_matrix) + group_terms(up_grad, up_matrix))
        return expert_out, slot_dx, down_grad

    expert_out, slot_dx, down_grad = lax.map(one_expert, (table, gate_weight, up_weight, down_weight))
    picked = expert_out.reshape(-1, D)[position].astype(jnp.float32).reshape(TOKENS, TOP, D)
    mixed_out = jnp.sum(picked * gate_weights[:, :, None], axis=1).astype(jnp.bfloat16)
    returned = slot_dx.reshape(-1, D)[position].astype(jnp.float32).reshape(TOKENS, TOP, D)
    input_grad = jnp.sum(returned, axis=1).astype(jnp.bfloat16)
    return mixed_out, input_grad, down_grad
```

```python
import functools

import jax
import jax.numpy as jnp
from jax import lax
from jax.experimental import pallas as pl
from jax.experimental.pallas import tpu as pltpu
from jax.sharding import PartitionSpec as P

MESH = pl.DeviceIdType.MESH
CAP = 2
PAD = 16
NX, NC = 4, 2
NY = 8
F32, BF16 = jnp.float32, jnp.bfloat16


def ring_offsets(n):
    out = [0]
    for k in range(1, n // 2 + 1):
        out.append(k)
        if k != n - k:
            out.append(n - k)
    return out


def nn(a, b):
    return lax.dot_general(a, b, (((1,), (0,)), ((), ())), preferred_element_type=F32)


def nt(a, b):
    return lax.dot_general(a, b, (((1,), (1,)), ((), ())), preferred_element_type=F32)


def tn(a, b, precision=None):
    return lax.dot_general(
        a, b, (((0,), (0,)), ((), ())), precision=precision, preferred_element_type=F32
    )


class Sems:
    def __init__(self):
        self.index = {}

    def at(self, key):
        return self.index.setdefault(key, len(self.index))


def kernel(nz, chunks, sizes, *refs):
    (hid, ids, gat, og, wg_hbm, wu_hbm, wd_hbm) = refs[:7]
    (mix_o, ing_o, dgr_o) = refs[7:10]
    (tok, rt, zs, g, wgu, dn, asc, csc, gsc, sel, selg, pre, agr, hact, gug, dgr) = refs[10:26]
    (pps, ppr, chip, d2r, nbr, fin, ret, ys, yr, send_sem, recv_sem, loc_sem) = refs[26:]
    token_count, width, hidden = sizes
    x_t = lax.axis_index("etp")
    x_e = lax.axis_index("expert")
    x, c = x_t // NC, x_t % NC
    z, y = x_e // NY, x_e % NY
    offs = ring_offsets(nz)
    group = NY * CAP
    rows = nz * group
    lanes = NY * PAD
    half = lanes // 2
    crow = rows // chunks
    per = nz // chunks
    slots = NX * NC

    def neg(p):
        return offs.index((nz - offs[p]) % nz)

    def zdev(p):
        return (lax.rem(z + offs[p], nz) * NY + y, x_t)

    def ydev(d):
        return (z * NY + lax.rem(y + d, NY), x_t)

    def tab(dx, other=0):
        return lax.rem(x + dx, NX) * NC + (1 - c if other else c)

    def xdev(dx):
        return (x_e, tab(dx))

    partner = (x_e, tab(0, 1))
    ssems, rsems, sends = Sems(), Sems(), []

    def put(src, dst, key_here, key_there, dev):
        copy = pltpu.make_async_remote_copy(
            src_ref=src,
            dst_ref=dst,
            send_sem=send_sem.at[ssems.at(key_here)],
            recv_sem=recv_sem.at[rsems.at(key_there)],
            device_id=dev,
            device_id_type=MESH,
        )
        copy.start()
        sends.append(copy)

    def got(dst, key, dev):
        pltpu.make_async_remote_copy(
            src_ref=dst,
            dst_ref=dst,
            send_sem=send_sem.at[0],
            recv_sem=recv_sem.at[rsems.at(key)],
            device_id=dev,
            device_id_type=MESH,
        ).wait_recv()

    loads = []
    for t in range(slots):
        cols = pl.ds(t * width, width)
        for src, dst in (
            (wg_hbm.at[cols, :], wgu.at[t, :, pl.ds(0, hidden)]),
            (wu_hbm.at[cols, :], wgu.at[t, :, pl.ds(hidden, hidden)]),
            (wd_hbm.at[:, cols], dn.at[t]),
        ):
            copy = pltpu.make_async_copy(src, dst, loc_sem.at[len(loads)])
            copy.start()
            loads.append(copy)

    peers = [zdev(p) for p in range(1, nz)] + [ydev(d) for d in range(1, NY)]
    peers += [xdev(1), xdev(3), partner]
    barrier = pltpu.get_barrier_semaphore()
    for dev in peers:
        pl.semaphore_signal(barrier, inc=1, device_id=dev, device_id_type=MESH)

    for k, src in ((0, hid), (1, og)):
        tok[k, 0:PAD, :] = jnp.zeros((PAD, width), BF16)
        tok[k, 0:token_count, :] = src[...]
    lane_t = lax.broadcasted_iota(jnp.int32, (token_count, lanes), 1)
    row_t = lax.broadcasted_iota(jnp.int32, (token_count, lanes), 0)
    here = lax.rem(lane_t, PAD) == row_t
    exact = lax.Precision.HIGHEST
    rt[0] = tn(ids[...].astype(F32), jnp.where(here & (lane_t < half), 1.0, 0.0), exact) + tn(
        gat[...], jnp.where(here & (lane_t >= half), 1.0, 0.0), exact
    )

    pl.semaphore_wait(barrier, len(peers))

    y_order = sorted(range(1, NY), key=lambda d: -min(d, NY - d))
    for d in y_order:
        put(rt.at[0], rt.at[NY - d], ("rt", d), ("rt", NY - d), ydev(d))
    for k in (0, 1):
        for d in y_order:
            put(
                tok.at[k, pl.ds(0, PAD)],
                tok.at[k, pl.ds((NY - d) * PAD, PAD)],
                ("tok", k, d),
                ("tok", k, NY - d),
                ydev(d),
            )

    for d in range(1, NY):
        got(rt.at[d], ("rt", d), ydev(d))
    lane8 = lax.broadcasted_iota(jnp.int32, rt.shape[1:], 1)
    ids_all = jnp.full(rt.shape[1:], -1.0, F32)
    gates_all = jnp.zeros(rt.shape[1:], F32)
    for d in range(NY):
        straight = rt[d]
        turned = pltpu.roll(straight, half, 1)
        mine = (lane8 // PAD == d) & (lax.rem(lane8, PAD) < token_count)
        low = d < NY // 2
        ids_all = jnp.where(mine, straight if low else turned, ids_all)
        gates_all = jnp.where(mine, turned if low else straight, gates_all)
    ids_all = ids_all.astype(jnp.int32)
    asc[...] = jnp.zeros(asc.shape, F32)
    for p in range(nz):
        hit = ids_all == lax.rem(z + offs[p], nz) * NY + y
        asc[p : p + 1, :] = jnp.sum(jnp.where(hit, 1.0, 0.0), axis=0, keepdims=True)
        gsc[p : p + 1, :] = jnp.sum(jnp.where(hit, gates_all, 0.0), axis=0, keepdims=True)
    l0 = lax.broadcasted_iota(jnp.int32, (lanes, lanes), 0)
    l1 = lax.broadcasted_iota(jnp.int32, (lanes, lanes), 1)
    earlier = jnp.where((l0 // PAD == l1 // PAD) & (l0 < l1), 1.0, 0.0).astype(BF16)
    csc[...] = nn(asc[...].astype(BF16), earlier)
    r2 = lax.broadcasted_iota(jnp.int32, (group, lanes), 0)
    b2 = lax.broadcasted_iota(jnp.int32, (group, lanes), 1) // PAD
    block = jnp.where(r2 // CAP == b2, 1.0, 0.0)
    rank = lax.rem(r2, CAP).astype(F32)
    for p in range(nz):
        pick = jnp.where(csc[p : p + 1, :] == rank, block, 0.0) * asc[p : p + 1, :]
        sel[p * group : (p + 1) * group, :] = pick.astype(BF16)
        selg[p * group : (p + 1) * group, :] = pick * gsc[p : p + 1, :]

    z_order = sorted(range(1, nz), key=lambda p: -p)
    for k in (0, 1):
        for d in range(1, NY):
            got(tok.at[k, pl.ds(d * PAD, PAD)], ("tok", k, d), ydev(d))
        picked = nn(sel[...], tok[k])
        if k == 1:
            picked = picked * jnp.sum(selg[...], axis=1, keepdims=True)
        zs[k] = picked.astype(BF16)
        for p in z_order:
            q = neg(p)
            put(
                zs.at[k, pl.ds(p * group, group)],
                g.at[k, x_t, pl.ds(q * group, group)],
                ("z", k, p),
                ("z", k, q),
                zdev(p),
            )
        g[k, x_t, 0:group, :] = zs[k, 0:group, :]

    for copy in loads:
        copy.wait()

    def piece(k, j, t):
        return g.at[k, t, pl.ds(j * crow, crow)]

    def pass_own(k, j):
        for p in range(j * per, (j + 1) * per):
            if p:
                got(g.at[k, x_t, pl.ds(p * group, group)], ("z", k, p), zdev(p))
        own = piece(k, j, x_t)
        put(own, own, ("g", k, j, "own+"), ("g", k, j, 3), xdev(1))
        put(own, own, ("g", k, j, "own-"), ("g", k, j, 1), xdev(3))
        put(own, own, ("g", k, j, "own|"), ("g", k, j, "o0"), partner)

    def pass_near(k, j):
        for dx in (3, 1):
            ref = piece(k, j, tab(dx))
            got(ref, ("g", k, j, dx), xdev(dx))
            if (j % 2 == 0) == (dx == 3):
                put(ref, ref, ("g", k, j, "far"), ("g", k, j, 2), xdev(4 - dx))
            put(ref, ref, ("g", k, j, "near|", dx), ("g", k, j, "o%d" % dx), partner)

    def pass_far(k, j):
        ref = piece(k, j, tab(2))
        got(ref, ("g", k, j, 2), xdev(3))
        put(ref, ref, ("g", k, j, "far|"), ("g", k, j, "o2"), partner)

    steps = [(k, j) for k in (0, 1) for j in range(chunks)]

    def step(s):
        if 0 <= s < len(steps):
            pass_own(*steps[s])
        if 0 <= s - 1 < len(steps):
            pass_near(*steps[s - 1])
        if 0 <= s - 2 < len(steps):
            pass_far(*steps[s - 2])

    def wait_other(k):
        for dx in (0, 3, 1, 2):
            for j in range(chunks):
                got(piece(k, j, tab(dx, 1)), ("g", k, j, "o%d" % dx), partner)

    for s in range(chunks + 2):
        step(s)
    pre[...] = nn(g[0, tab(0)], wgu[tab(0)])
    for dx in (3, 1, 2):
        pre[...] += nn(g[0, tab(dx)], wgu[tab(dx)])
    wait_other(0)
    for dx in (0, 3, 1, 2):
        pre[...] += nn(g[0, tab(dx, 1)], wgu[tab(dx, 1)])
    gate_pre, up_pre = pre[:, 0:hidden], pre[:, hidden : 2 * hidden]
    hact[...] = (gate_pre * jax.nn.sigmoid(gate_pre) * up_pre).astype(BF16)

    def part(k, t):
        return nn(hact[...], dn[t]) if k == 0 else nt(gug[...], wgu[t])

    order = (2, 1, 3, 0)

    def reduce_pair_send(k):
        for dx in order:
            pps[k, dx] = part(k, tab(dx, 1)).astype(BF16)
            put(pps.at[k, dx], ppr.at[k, dx], ("pp", k, dx), ("pp", k, dx), partner)

    first, second = pl.ds(0, rows // 2), pl.ds(rows // 2, rows // 2)

    def reduce_pair(k, dx):
        mine = part(k, tab(dx))
        got(ppr.at[k, dx], ("pp", k, dx), partner)
        chip[k, dx] = (mine + ppr[k, dx].astype(F32)).astype(BF16)

    def reduce_start(k):
        reduce_pair(k, 2)
        put(chip.at[k, 2, first], d2r.at[k, 0], ("d2", k, 0), ("d2", k, 0), xdev(1))
        put(chip.at[k, 2, second], d2r.at[k, 1], ("d2", k, 1), ("d2", k, 1), xdev(3))
        reduce_pair(k, 1)
        put(chip.at[k, 1, second], nbr.at[k, 0, second], ("n", k, 0, 1), ("n", k, 0, 1), xdev(1))
        reduce_pair(k, 3)
        put(chip.at[k, 3, first], nbr.at[k, 1, first], ("n", k, 1, 0), ("n", k, 1, 0), xdev(3))
        reduce_pair(k, 0)

    def reduce_relay(k):
        for i, (dx, part_rows) in enumerate(((1, first), (3, second))):
            got(d2r.at[k, i], ("d2", k, i), xdev(4 - dx))
            chip[k, dx, part_rows] = (
                chip[k, dx, part_rows].astype(F32) + d2r[k, i].astype(F32)
            ).astype(BF16)
            put(
                chip.at[k, dx, part_rows],
                nbr.at[k, i, part_rows],
                ("n", k, i, i),
                ("n", k, i, i),
                xdev(dx),
            )

    def reduce_end(k):
        for i in (0, 1):
            for h, part_rows in enumerate((first, second)):
                got(nbr.at[k, i, part_rows], ("n", k, i, h), xdev(3 if i == 0 else 1))
        fin[k] = (
            chip[k, 0].astype(F32) + nbr[k, 0].astype(F32) + nbr[k, 1].astype(F32)
        ).astype(BF16)
        for p in z_order:
            q = neg(p)
            put(
                fin.at[k, pl.ds(p * group, group)],
                ret.at[k, pl.ds(q * group, group)],
                ("back", k, p),
                ("back", k, q),
                zdev(p),
            )
        ret[k, 0:group, :] = fin[k, 0:group, :]

    reduce_pair_send(0)
    step(chunks + 2)
    step(chunks + 3)
    reduce_start(0)
    for s in range(chunks + 4, 2 * chunks + 2):
        step(s)

    agr[...] = nt(g[1, tab(0)], dn[tab(0)])
    for dx in (3, 1, 2):
        agr[...] += nt(g[1, tab(dx)], dn[tab(dx)])
    wait_other(1)
    for dx in (0, 3, 1, 2):
        agr[...] += nt(g[1, tab(dx, 1)], dn[tab(dx, 1)])
    gate_pre, up_pre = pre[:, 0:hidden], pre[:, hidden : 2 * hidden]
    sig = jax.nn.sigmoid(gate_pre)
    act_grad = agr[...]
    gug[:, 0:hidden] = (act_grad * up_pre * sig * (1.0 + gate_pre * (1.0 - sig))).astype(BF16)
    gug[:, hidden : 2 * hidden] = (act_grad * (gate_pre * sig)).astype(BF16)

    reduce_pair_send(1)
    reduce_relay(0)
    reduce_start(1)
    reduce_end(0)
    reduce_relay(1)

    for t in range(slots):
        dgr[:, t * width : (t + 1) * width] = tn(hact[...], g[1, t]).astype(BF16)
    dgr_copy = pltpu.make_async_copy(dgr, dgr_o, loc_sem.at[0])
    dgr_copy.start()

    def combine(k):
        for p in range(1, nz):
            got(ret.at[k, pl.ds(p * group, group)], ("back", k, p), zdev(p))
        if k == 0:
            coarse = selg[...].astype(BF16)
            fine = (selg[...] - coarse.astype(F32)).astype(BF16)
            summed = tn(coarse, ret[k]) + tn(fine, ret[k])
        else:
            summed = tn(sel[...], ret[k])
        ys[k] = summed.astype(BF16)
        for d in y_order:
            put(
                ys.at[k, pl.ds(d * PAD, PAD)],
                yr.at[k, NY - d],
                ("ys", k, d),
                ("ys", k, NY - d),
                ydev(d),
            )

    def finish(k, out):
        total = ys[k, 0:PAD, :].astype(F32)
        for d in range(1, NY):
            got(yr.at[k, d], ("ys", k, d), ydev(d))
            total = total + yr[k, d].astype(F32)
        out[...] = total[0:token_count, :].astype(BF16)

    combine(0)
    reduce_end(1)
    finish(0, mix_o)
    combine(1)
    finish(1, ing_o)

    dgr_copy.wait()
    for copy in sends:
        copy.wait_send()
    assert len(ssems.index) <= send_sem.shape[0] and len(rsems.index) <= recv_sem.shape[0]


def on_device(hidden_in, expert_ids, gate_weights, out_grad, gate_weight, up_weight, down_weight):
    token_count, per_token = expert_ids.shape
    nz = lax.axis_size("expert") // NY
    width = hidden_in.shape[1]
    hidden = gate_weight.shape[2]
    slots = NX * NC
    rows = nz * NY * CAP
    lanes = NY * PAD
    chunks = 4 if nz % 4 == 0 else 2
    copies = 2 * (NY - 1) * 3 + 4 * (nz - 1) + 2 * 7 * chunks + 64
    vmem = pl.BlockSpec(memory_space=pltpu.VMEM)
    hbm = pl.BlockSpec(memory_space=pl.ANY)
    mixed, input_grad, down_grad = pl.pallas_call(
        functools.partial(kernel, nz, chunks, (token_count, width, hidden)),
        out_shape=(
            jax.ShapeDtypeStruct((token_count, width), BF16),
            jax.ShapeDtypeStruct((token_count, width), BF16),
            jax.ShapeDtypeStruct((hidden, slots * width), BF16),
        ),
        in_specs=[vmem] * 4 + [hbm] * 3,
        out_specs=(vmem, vmem, hbm),
        scratch_shapes=[
            pltpu.VMEM((2, lanes, width), BF16),
            pltpu.VMEM((NY, per_token, lanes), F32),
            pltpu.VMEM((2, rows, width), BF16),
            pltpu.VMEM((2, slots, rows, width), BF16),
            pltpu.VMEM((slots, width, 2 * hidden), BF16),
            pltpu.VMEM((slots, hidden, width), BF16),
            pltpu.VMEM((16, lanes), F32),
            pltpu.VMEM((16, lanes), F32),
            pltpu.VMEM((16, lanes), F32),
            pltpu.VMEM((rows, lanes), BF16),
            pltpu.VMEM((rows, lanes), F32),
            pltpu.VMEM((rows, 2 * hidden), F32),
            pltpu.VMEM((rows, hidden), F32),
            pltpu.VMEM((rows, hidden), BF16),
            pltpu.VMEM((rows, 2 * hidden), BF16),
            pltpu.VMEM((hidden, slots * width), BF16),
            pltpu.VMEM((2, NX, rows, width), BF16),
            pltpu.VMEM((2, NX, rows, width), BF16),
            pltpu.VMEM((2, NX, rows, width), BF16),
            pltpu.VMEM((2, 2, rows // 2, width), BF16),
            pltpu.VMEM((2, 2, rows, width), BF16),
            pltpu.VMEM((2, rows, width), BF16),
            pltpu.VMEM((2, rows, width), BF16),
            pltpu.VMEM((2, lanes, width), BF16),
            pltpu.VMEM((2, NY, PAD, width), BF16),
            pltpu.SemaphoreType.DMA((copies,)),
            pltpu.SemaphoreType.DMA((copies,)),
            pltpu.SemaphoreType.DMA((3 * slots,)),
        ],
        compiler_params=pltpu.CompilerParams(
            collective_id=0, has_side_effects=True, vmem_limit_bytes=48 << 20
        ),
    )(hidden_in, expert_ids, gate_weights, out_grad, gate_weight[0], up_weight[0], down_weight[0])
    return mixed, input_grad, down_grad[None]


def solution(mesh):
    return jax.shard_map(
        on_device,
        mesh=mesh,
        in_specs=(
            P("expert", "etp"),
            P("expert", None),
            P("expert", None),
            P("expert", "etp"),
            P("expert", None, "etp"),
            P("expert", None, "etp"),
            P("expert", "etp", None),
        ),
        out_specs=(P("expert", "etp"), P("expert", "etp"), P("expert", "etp", None)),
        check_vma=False,
    )
```

```python
import functools

import jax
import jax.numpy as jnp
from jax import lax
from jax.experimental import pallas as pl
from jax.experimental.pallas import tpu as pltpu
from jax.sharding import PartitionSpec as P

MESH = pl.DeviceIdType.MESH
CAP = 2
PAD = 16
NX, NC = 4, 2
NY = 8
F32, BF16 = jnp.float32, jnp.bfloat16


def ring_offsets(n):
    out = [0]
    for k in range(1, n // 2 + 1):
        out.append(k)
        if k != n - k:
            out.append(n - k)
    return out


def nn(a, b, precision=None):
    return lax.dot_general(
        a, b, (((1,), (0,)), ((), ())), precision=precision, preferred_element_type=F32
    )


def nt(a, b):
    return lax.dot_general(a, b, (((1,), (1,)), ((), ())), preferred_element_type=F32)


def tn(a, b):
    return lax.dot_general(a, b, (((0,), (0,)), ((), ())), preferred_element_type=F32)


class Sems:
    def __init__(self):
        self.index = {}

    def at(self, key):
        return self.index.setdefault(key, len(self.index))


def kernel(nz, chunks, sizes, *refs):
    (hid_hbm, ids_hbm, gat_hbm, og_hbm, wg_hbm, wu_hbm, wd_hbm) = refs[:7]
    (mix_o, ing_o, dgr_o) = refs[7:10]
    (hid, ids, gat, og, tok, rt, zs, g, wgu, dn, asc, csc, gsc, sel, selg, pre, agr, hact, gug, dgr) = refs[10:30]
    (pps, ppr, chip, d2r, nbr, fin, ret, ys, yr, send_sem, recv_sem, loc_sem) = refs[30:]
    token_count, width, hidden = sizes
    x_t = lax.axis_index("etp")
    x_e = lax.axis_index("expert")
    x, c = x_t // NC, x_t % NC
    z, y = x_e // NY, x_e % NY
    offs = ring_offsets(nz)
    group = NY * CAP
    rows = nz * group
    lanes = NY * PAD
    half = lanes // 2
    crow = rows // chunks
    per = nz // chunks
    slots = NX * NC

    def neg(p):
        return offs.index((nz - offs[p]) % nz)

    def zdev(p):
        return (lax.rem(z + offs[p], nz) * NY + y, x_t)

    def ydev(d):
        return (z * NY + lax.rem(y + d, NY), x_t)

    def tab(dx, other=0):
        return lax.rem(x + dx, NX) * NC + (1 - c if other else c)

    def xdev(dx):
        return (x_e, tab(dx))

    partner = (x_e, tab(0, 1))
    ssems, rsems, sends = Sems(), Sems(), []

    def put(src, dst, key_here, key_there, dev):
        copy = pltpu.make_async_remote_copy(
            src_ref=src,
            dst_ref=dst,
            send_sem=send_sem.at[ssems.at(key_here)],
            recv_sem=recv_sem.at[rsems.at(key_there)],
            device_id=dev,
            device_id_type=MESH,
        )
        copy.start()
        sends.append(copy)

    def got(dst, key, dev):
        pltpu.make_async_remote_copy(
            src_ref=dst,
            dst_ref=dst,
            send_sem=send_sem.at[0],
            recv_sem=recv_sem.at[rsems.at(key)],
            device_id=dev,
            device_id_type=MESH,
        ).wait_recv()

    small, loads = [], []
    for i, (src, dst) in enumerate(((ids_hbm, ids), (gat_hbm, gat), (hid_hbm, hid), (og_hbm, og))):
        copy = pltpu.make_async_copy(src, dst, loc_sem.at[3 * slots + i])
        copy.start()
        small.append(copy)
    for t in range(slots):
        cols = pl.ds(t * width, width)
        for src, dst in (
            (wg_hbm.at[cols, :], wgu.at[t, :, pl.ds(0, hidden)]),
            (wu_hbm.at[cols, :], wgu.at[t, :, pl.ds(hidden, hidden)]),
            (wd_hbm.at[:, cols], dn.at[t]),
        ):
            copy = pltpu.make_async_copy(src, dst, loc_sem.at[len(loads)])
            copy.start()
            loads.append(copy)

    peers = [zdev(p) for p in range(1, nz)] + [ydev(d) for d in range(1, NY)]
    peers += [xdev(1), xdev(3), partner]
    barrier = pltpu.get_barrier_semaphore()
    for dev in peers:
        pl.semaphore_signal(barrier, inc=1, device_id=dev, device_id_type=MESH)

    for copy in small:
        copy.wait()
    for k, src in ((0, hid), (1, og)):
        tok[k, 0:PAD, :] = jnp.zeros((PAD, width), BF16)
        tok[k, 0:token_count, :] = src[...]
    lane_t = lax.broadcasted_iota(jnp.int32, (token_count, lanes), 1)
    row_t = lax.broadcasted_iota(jnp.int32, (token_count, lanes), 0)
    here = lax.rem(lane_t, PAD) == row_t
    exact = lax.Precision.HIGHEST
    rt[0] = nn(ids[...].astype(F32), jnp.where(here & (lane_t < half), 1.0, 0.0), exact) + nn(
        gat[...], jnp.where(here & (lane_t >= half), 1.0, 0.0), exact
    )

    pl.semaphore_wait(barrier, len(peers))

    y_order = sorted(range(1, NY), key=lambda d: -min(d, NY - d))
    for d in y_order:
        put(rt.at[0], rt.at[NY - d], ("rt", d), ("rt", NY - d), ydev(d))
    for k in (0, 1):
        for d in y_order:
            put(
                tok.at[k, pl.ds(0, PAD)],
                tok.at[k, pl.ds((NY - d) * PAD, PAD)],
                ("tok", k, d),
                ("tok", k, NY - d),
                ydev(d),
            )

    for d in range(1, NY):
        got(rt.at[d], ("rt", d), ydev(d))
    lane8 = lax.broadcasted_iota(jnp.int32, rt.shape[1:], 1)
    ids_all = jnp.full(rt.shape[1:], -1.0, F32)
    gates_all = jnp.zeros(rt.shape[1:], F32)
    for d in range(NY):
        straight = rt[d]
        turned = pltpu.roll(straight, half, 1)
        mine = (lane8 // PAD == d) & (lax.rem(lane8, PAD) < token_count)
        low = d < NY // 2
        ids_all = jnp.where(mine, straight if low else turned, ids_all)
        gates_all = jnp.where(mine, turned if low else straight, gates_all)
    ids_all = ids_all.astype(jnp.int32)
    asc[...] = jnp.zeros(asc.shape, F32)
    for p in range(nz):
        hit = ids_all == lax.rem(z + offs[p], nz) * NY + y
        asc[p : p + 1, :] = jnp.sum(jnp.where(hit, 1.0, 0.0), axis=0, keepdims=True)
        gsc[p : p + 1, :] = jnp.sum(jnp.where(hit, gates_all, 0.0), axis=0, keepdims=True)
    l0 = lax.broadcasted_iota(jnp.int32, (lanes, lanes), 0)
    l1 = lax.broadcasted_iota(jnp.int32, (lanes, lanes), 1)
    earlier = jnp.where((l0 // PAD == l1 // PAD) & (l0 < l1), 1.0, 0.0).astype(BF16)
    csc[...] = nn(asc[...].astype(BF16), earlier)
    r2 = lax.broadcasted_iota(jnp.int32, (group, lanes), 0)
    b2 = lax.broadcasted_iota(jnp.int32, (group, lanes), 1) // PAD
    block = jnp.where(r2 // CAP == b2, 1.0, 0.0)
    rank = lax.rem(r2, CAP).astype(F32)
    for p in range(nz):
        pick = jnp.where(csc[p : p + 1, :] == rank, block, 0.0) * asc[p : p + 1, :]
        sel[p * group : (p + 1) * group, :] = pick.astype(BF16)
        selg[p * group : (p + 1) * group, :] = pick * gsc[p : p + 1, :]

    z_order = range(1, nz)
    for k in (0, 1):
        for d in range(1, NY):
            got(tok.at[k, pl.ds(d * PAD, PAD)], ("tok", k, d), ydev(d))
        picked = nn(sel[...], tok[k])
        if k == 1:
            picked = picked * jnp.sum(selg[...], axis=1, keepdims=True)
        zs[k] = picked.astype(BF16)
        for p in z_order:
            q = neg(p)
            put(
                zs.at[k, pl.ds(p * group, group)],
                g.at[k, x_t, pl.ds(q * group, group)],
                ("z", k, p),
                ("z", k, q),
                zdev(p),
            )
        g[k, x_t, 0:group, :] = zs[k, 0:group, :]

    for copy in loads:
        copy.wait()

    def piece(k, j, t):
        return g.at[k, t, pl.ds(j * crow, crow)]

    def pass_own(k, j):
        for p in range(j * per, (j + 1) * per):
            if p:
                got(g.at[k, x_t, pl.ds(p * group, group)], ("z", k, p), zdev(p))
        own = piece(k, j, x_t)
        put(own, own, ("g", k, j, "own+"), ("g", k, j, 3), xdev(1))
        put(own, own, ("g", k, j, "own-"), ("g", k, j, 1), xdev(3))
        put(own, own, ("g", k, j, "own|"), ("g", k, j, "o0"), partner)

    def pass_near(k, j):
        for dx in (3, 1):
            ref = piece(k, j, tab(dx))
            got(ref, ("g", k, j, dx), xdev(dx))
            if (j % 2 == 0) == (dx == 3):
                put(ref, ref, ("g", k, j, "far"), ("g", k, j, 2), xdev(4 - dx))
            put(ref, ref, ("g", k, j, "near|", dx), ("g", k, j, "o%d" % dx), partner)

    def pass_far(k, j):
        ref = piece(k, j, tab(2))
        got(ref, ("g", k, j, 2), xdev(3))
        put(ref, ref, ("g", k, j, "far|"), ("g", k, j, "o2"), partner)

    steps = [(k, j) for k in (0, 1) for j in range(chunks)]

    def step(s):
        for wait, pass_on in ((s, pass_own), (s - 4, pass_far), (s - 2, pass_near)):
            if 0 <= wait < len(steps):
                pass_on(*steps[wait])

    def wait_other(k):
        for dx in (0, 3, 1, 2):
            for j in range(chunks):
                got(piece(k, j, tab(dx, 1)), ("g", k, j, "o%d" % dx), partner)

    for s in range(chunks):
        step(s)
    pre[...] = nn(g[0, tab(0)], wgu[tab(0)])
    for s in range(chunks, chunks + 2):
        step(s)
    for dx in (3, 1):
        pre[...] += nn(g[0, tab(dx)], wgu[tab(dx)])
    for s in range(chunks + 2, 2 * chunks):
        step(s)
    pre[...] += nn(g[0, tab(2)], wgu[tab(2)])
    wait_other(0)
    for dx in (0, 3, 1, 2):
        pre[...] += nn(g[0, tab(dx, 1)], wgu[tab(dx, 1)])
    gate_pre, up_pre = pre[:, 0:hidden], pre[:, hidden : 2 * hidden]
    hact[...] = (gate_pre * jax.nn.sigmoid(gate_pre) * up_pre).astype(BF16)

    def span(h):
        return pl.ds(h * (rows // 2), rows // 2)

    left, right = pl.ds(0, width // 2), pl.ds(width // 2, width // 2)

    def part(k, h, t):
        if k == 0:
            return nn(hact[span(h), :], dn[t])
        return nt(gug[span(h), :], wgu[t])

    def pair_send(k, h, dx):
        pps[k, dx, span(h), :] = part(k, h, tab(dx, 1)).astype(BF16)
        put(
            pps.at[k, dx, span(h)],
            ppr.at[k, dx, span(h)],
            ("pp", k, h, dx),
            ("pp", k, h, dx),
            partner,
        )

    def pair_sum(k, h, dx):
        mine = part(k, h, tab(dx))
        got(ppr.at[k, dx, span(h)], ("pp", k, h, dx), partner)
        chip[k, dx, span(h), :] = (mine + ppr[k, dx, span(h), :].astype(F32)).astype(BF16)
        if dx == 2:
            for i, (cols, to) in enumerate(((left, 1), (right, 3))):
                put(
                    chip.at[k, 2, span(h), cols],
                    d2r.at[k, i, span(h)],
                    ("d2", k, h, i),
                    ("d2", k, h, i),
                    xdev(to),
                )
        elif dx:
            i, cols = (0, right) if dx == 1 else (1, left)
            put(
                chip.at[k, dx, span(h), cols],
                nbr.at[k, i, span(h), cols],
                ("n", k, h, i, "direct"),
                ("n", k, h, i, "direct"),
                xdev(dx),
            )

    def reduce_start(k, h):
        pair_send(k, h, 2)
        pair_send(k, h, 1)
        pair_sum(k, h, 2)
        pair_send(k, h, 3)
        pair_sum(k, h, 1)
        pair_send(k, h, 0)
        pair_sum(k, h, 3)
        pair_sum(k, h, 0)

    def reduce_relay(k, h):
        for i, (dx, cols) in enumerate(((1, left), (3, right))):
            got(d2r.at[k, i, span(h)], ("d2", k, h, i), xdev(4 - dx))
            chip[k, dx, span(h), cols] = (
                chip[k, dx, span(h), cols].astype(F32) + d2r[k, i, span(h), :].astype(F32)
            ).astype(BF16)
            put(
                chip.at[k, dx, span(h), cols],
                nbr.at[k, i, span(h), cols],
                ("n", k, h, i, "relay"),
                ("n", k, h, i, "relay"),
                xdev(dx),
            )

    def reduce_end(k, h):
        for i, (direct, relayed) in enumerate(((right, left), (left, right))):
            came = xdev(3 if i == 0 else 1)
            got(nbr.at[k, i, span(h), direct], ("n", k, h, i, "direct"), came)
            got(nbr.at[k, i, span(h), relayed], ("n", k, h, i, "relay"), came)
        fin[k, span(h), :] = (
            chip[k, 0, span(h), :].astype(F32)
            + nbr[k, 0, span(h), :].astype(F32)
            + nbr[k, 1, span(h), :].astype(F32)
        ).astype(BF16)
        for p in range(h * (nz // 2), (h + 1) * (nz // 2)):
            if p == 0:
                continue
            q = neg(p)
            put(
                fin.at[k, pl.ds(p * group, group)],
                ret.at[k, pl.ds(q * group, group)],
                ("back", k, p),
                ("back", k, q),
                zdev(p),
            )
        if h == 0:
            ret[k, 0:group, :] = fin[k, 0:group, :]

    reduce_start(0, 1)
    step(2 * chunks)
    step(2 * chunks + 1)
    reduce_start(0, 0)
    step(2 * chunks + 2)
    step(2 * chunks + 3)
    reduce_relay(0, 1)

    agr[...] = nt(g[1, tab(0)], dn[tab(0)])
    for dx in (3, 1, 2):
        agr[...] += nt(g[1, tab(dx)], dn[tab(dx)])
    reduce_relay(0, 0)
    wait_other(1)
    for dx in (0, 3, 1, 2):
        agr[...] += nt(g[1, tab(dx, 1)], dn[tab(dx, 1)])
    gate_pre, up_pre = pre[:, 0:hidden], pre[:, hidden : 2 * hidden]
    sig = jax.nn.sigmoid(gate_pre)
    act_grad = agr[...]
    gug[:, 0:hidden] = (act_grad * up_pre * sig * (1.0 + gate_pre * (1.0 - sig))).astype(BF16)
    gug[:, hidden : 2 * hidden] = (act_grad * (gate_pre * sig)).astype(BF16)

    reduce_start(1, 1)
    reduce_end(0, 1)
    reduce_start(1, 0)
    reduce_end(0, 0)
    reduce_relay(1, 1)

    def weight_grad(t):
        dgr[:, t * width : (t + 1) * width] = tn(hact[...], g[1, t]).astype(BF16)

    for t in range(slots // 2):
        weight_grad(t)
    reduce_relay(1, 0)
    for t in range(slots // 2, slots):
        weight_grad(t)
    dgr_copy = pltpu.make_async_copy(dgr, dgr_o, loc_sem.at[0])
    dgr_copy.start()

    def combine(k):
        for p in range(1, nz):
            got(ret.at[k, pl.ds(p * group, group)], ("back", k, p), zdev(p))
        if k == 0:
            coarse = selg[...].astype(BF16)
            fine = (selg[...] - coarse.astype(F32)).astype(BF16)
            summed = tn(coarse, ret[k]) + tn(fine, ret[k])
        else:
            summed = tn(sel[...], ret[k])
        ys[k] = summed.astype(BF16)
        for d in y_order:
            put(
                ys.at[k, pl.ds(d * PAD, PAD)],
                yr.at[k, NY - d],
                ("ys", k, d),
                ("ys", k, NY - d),
                ydev(d),
            )

    def finish(k, out):
        total = ys[k, 0:PAD, :].astype(F32)
        for d in range(1, NY):
            got(yr.at[k, d], ("ys", k, d), ydev(d))
            total = total + yr[k, d].astype(F32)
        out[...] = total[0:token_count, :].astype(BF16)

    reduce_end(1, 1)
    combine(0)
    reduce_end(1, 0)
    combine(1)
    finish(0, mix_o)
    finish(1, ing_o)

    dgr_copy.wait()
    for copy in sends:
        copy.wait_send()
    assert len(ssems.index) <= send_sem.shape[0] and len(rsems.index) <= recv_sem.shape[0]


def on_device(hidden_in, expert_ids, gate_weights, out_grad, gate_weight, up_weight, down_weight):
    token_count, per_token = expert_ids.shape
    nz = lax.axis_size("expert") // NY
    width = hidden_in.shape[1]
    hidden = gate_weight.shape[2]
    slots = NX * NC
    rows = nz * NY * CAP
    lanes = NY * PAD
    chunks = 4 if nz % 4 == 0 else 2
    copies = 2 * (NY - 1) * 3 + 4 * (nz - 1) + 2 * 7 * chunks + 96
    vmem = pl.BlockSpec(memory_space=pltpu.VMEM)
    hbm = pl.BlockSpec(memory_space=pltpu.HBM)
    mixed, input_grad, down_grad = pl.pallas_call(
        functools.partial(kernel, nz, chunks, (token_count, width, hidden)),
        out_shape=(
            jax.ShapeDtypeStruct((token_count, width), BF16),
            jax.ShapeDtypeStruct((token_count, width), BF16),
            jax.ShapeDtypeStruct((hidden, slots * width), BF16),
        ),
        in_specs=[hbm] * 7,
        out_specs=(vmem, vmem, hbm),
        scratch_shapes=[
            pltpu.VMEM((token_count, width), BF16),
            pltpu.VMEM((per_token, token_count), jnp.int32),
            pltpu.VMEM((per_token, token_count), F32),
            pltpu.VMEM((token_count, width), BF16),
            pltpu.VMEM((2, lanes, width), BF16),
            pltpu.VMEM((NY, per_token, lanes), F32),
            pltpu.VMEM((2, rows, width), BF16),
            pltpu.VMEM((2, slots, rows, width), BF16),
            pltpu.VMEM((slots, width, 2 * hidden), BF16),
            pltpu.VMEM((slots, hidden, width), BF16),
            pltpu.VMEM((16, lanes), F32),
            pltpu.VMEM((16, lanes), F32),
            pltpu.VMEM((16, lanes), F32),
            pltpu.VMEM((rows, lanes), BF16),
            pltpu.VMEM((rows, lanes), F32),
            pltpu.VMEM((rows, 2 * hidden), F32),
            pltpu.VMEM((rows, hidden), F32),
            pltpu.VMEM((rows, hidden), BF16),
            pltpu.VMEM((rows, 2 * hidden), BF16),
            pltpu.VMEM((hidden, slots * width), BF16),
            pltpu.VMEM((2, NX, rows, width), BF16),
            pltpu.VMEM((2, NX, rows, width), BF16),
            pltpu.VMEM((2, NX, rows, width), BF16),
            pltpu.VMEM((2, 2, rows, width // 2), BF16),
            pltpu.VMEM((2, 2, rows, width), BF16),
            pltpu.VMEM((2, rows, width), BF16),
            pltpu.VMEM((2, rows, width), BF16),
            pltpu.VMEM((2, lanes, width), BF16),
            pltpu.VMEM((2, NY, PAD, width), BF16),
            pltpu.SemaphoreType.DMA((copies,)),
            pltpu.SemaphoreType.DMA((copies,)),
            pltpu.SemaphoreType.DMA((3 * slots + 4,)),
        ],
        compiler_params=pltpu.CompilerParams(
            collective_id=0, has_side_effects=True, vmem_limit_bytes=48 << 20
        ),
    )(
        *(
            pltpu.with_memory_space_constraint(a, pltpu.HBM)
            for a in (
                hidden_in,
                expert_ids.T,
                gate_weights.T,
                out_grad,
                gate_weight[0],
                up_weight[0],
                down_weight[0],
            )
        )
    )
    return mixed, input_grad, down_grad[None]


def solution(mesh):
    return jax.shard_map(
        on_device,
        mesh=mesh,
        in_specs=(
            P("expert", "etp"),
            P("expert", None),
            P("expert", None),
            P("expert", "etp"),
            P("expert", None, "etp"),
            P("expert", None, "etp"),
            P("expert", "etp", None),
        ),
        out_specs=(P("expert", "etp"), P("expert", "etp"), P("expert", "etp", None)),
        check_vma=False,
    )
```

```python
import functools

import jax
import jax.numpy as jnp
from jax import lax
from jax.experimental import pallas as pl
from jax.experimental.pallas import tpu as pltpu
from jax.sharding import PartitionSpec as P

MESH = pl.DeviceIdType.MESH
CAP = 2
PAD = 16
NX, NC = 4, 2
NY = 8
F32, BF16 = jnp.float32, jnp.bfloat16


def ring_offsets(n):
    out = [0]
    for k in range(1, n // 2 + 1):
        out.append(k)
        if k != n - k:
            out.append(n - k)
    return out


def nn(a, b, precision=None):
    return lax.dot_general(
        a, b, (((1,), (0,)), ((), ())), precision=precision, preferred_element_type=F32
    )


def nt(a, b):
    return lax.dot_general(a, b, (((1,), (1,)), ((), ())), preferred_element_type=F32)


def tn(a, b):
    return lax.dot_general(a, b, (((0,), (0,)), ((), ())), preferred_element_type=F32)


class Sems:
    def __init__(self):
        self.index = {}

    def at(self, key):
        return self.index.setdefault(key, len(self.index))


def kernel(nz, chunks, sizes, *refs):
    (hid_hbm, ids_hbm, gat_hbm, og_hbm, wg_hbm, wu_hbm, wd_hbm) = refs[:7]
    (mix_o, ing_o, dgr_o) = refs[7:10]
    (hid, ids, gat, og, tok, rt, zs, g, wgu, dn, asc, csc, gsc, sel, selg, pre, agr, hact, gug, dgr) = refs[10:30]
    (pps, ppr, chip, nbr, fin, ret, ys, yr, send_sem, recv_sem, loc_sem) = refs[30:]
    token_count, width, hidden = sizes
    x_t = lax.axis_index("etp")
    x_e = lax.axis_index("expert")
    x, c = x_t // NC, x_t % NC
    z, y = x_e // NY, x_e % NY
    offs = ring_offsets(nz)
    group = NY * CAP
    rows = nz * group
    lanes = NY * PAD
    half = lanes // 2
    crow = rows // chunks
    per = nz // chunks
    slots = NX * NC

    def neg(p):
        return offs.index((nz - offs[p]) % nz)

    def zdev(p):
        return (lax.rem(z + offs[p], nz) * NY + y, x_t)

    def ydev(d):
        return (z * NY + lax.rem(y + d, NY), x_t)

    def tab(dx, other=0):
        return lax.rem(x + dx, NX) * NC + (1 - c if other else c)

    def xdev(dx):
        return (x_e, tab(dx))

    partner = (x_e, tab(0, 1))
    ssems, rsems, sends = Sems(), Sems(), []

    def put(src, dst, key_here, key_there, dev):
        copy = pltpu.make_async_remote_copy(
            src_ref=src,
            dst_ref=dst,
            send_sem=send_sem.at[ssems.at(key_here)],
            recv_sem=recv_sem.at[rsems.at(key_there)],
            device_id=dev,
            device_id_type=MESH,
        )
        copy.start()
        sends.append(copy)

    def got(dst, key, dev):
        pltpu.make_async_remote_copy(
            src_ref=dst,
            dst_ref=dst,
            send_sem=send_sem.at[0],
            recv_sem=recv_sem.at[rsems.at(key)],
            device_id=dev,
            device_id_type=MESH,
        ).wait_recv()

    small, loads = [], []
    for i, (src, dst) in enumerate(((ids_hbm, ids), (gat_hbm, gat), (hid_hbm, hid), (og_hbm, og))):
        copy = pltpu.make_async_copy(src, dst, loc_sem.at[3 * slots + i])
        copy.start()
        small.append(copy)
    for t in range(slots):
        cols = pl.ds(t * width, width)
        for src, dst in (
            (wg_hbm.at[cols, :], wgu.at[t, :, pl.ds(0, hidden)]),
            (wu_hbm.at[cols, :], wgu.at[t, :, pl.ds(hidden, hidden)]),
            (wd_hbm.at[:, cols], dn.at[t]),
        ):
            copy = pltpu.make_async_copy(src, dst, loc_sem.at[len(loads)])
            copy.start()
            loads.append(copy)

    peers = [zdev(p) for p in range(1, nz)] + [ydev(d) for d in range(1, NY)]
    peers += [xdev(1), xdev(2), xdev(3), partner]
    barrier = pltpu.get_barrier_semaphore()
    for dev in peers:
        pl.semaphore_signal(barrier, inc=1, device_id=dev, device_id_type=MESH)

    for copy in small:
        copy.wait()
    for k, src in ((0, hid), (1, og)):
        tok[k, 0:PAD, :] = jnp.zeros((PAD, width), BF16)
        tok[k, 0:token_count, :] = src[...]
    lane_t = lax.broadcasted_iota(jnp.int32, (token_count, lanes), 1)
    row_t = lax.broadcasted_iota(jnp.int32, (token_count, lanes), 0)
    here = lax.rem(lane_t, PAD) == row_t
    exact = lax.Precision.HIGHEST
    rt[0] = nn(ids[...].astype(F32), jnp.where(here & (lane_t < half), 1.0, 0.0), exact) + nn(
        gat[...], jnp.where(here & (lane_t >= half), 1.0, 0.0), exact
    )

    pl.semaphore_wait(barrier, len(peers))

    y_order = sorted(range(1, NY), key=lambda d: -min(d, NY - d))
    for d in y_order:
        put(rt.at[0], rt.at[NY - d], ("rt", d), ("rt", NY - d), ydev(d))
    for k in (0, 1):
        for d in y_order:
            put(
                tok.at[k, pl.ds(0, PAD)],
                tok.at[k, pl.ds((NY - d) * PAD, PAD)],
                ("tok", k, d),
                ("tok", k, NY - d),
                ydev(d),
            )

    for d in range(1, NY):
        got(rt.at[d], ("rt", d), ydev(d))
    lane8 = lax.broadcasted_iota(jnp.int32, rt.shape[1:], 1)
    ids_all = jnp.full(rt.shape[1:], -1.0, F32)
    gates_all = jnp.zeros(rt.shape[1:], F32)
    for d in range(NY):
        straight = rt[d]
        turned = pltpu.roll(straight, half, 1)
        mine = (lane8 // PAD == d) & (lax.rem(lane8, PAD) < token_count)
        low = d < NY // 2
        ids_all = jnp.where(mine, straight if low else turned, ids_all)
        gates_all = jnp.where(mine, turned if low else straight, gates_all)
    ids_all = ids_all.astype(jnp.int32)
    asc[...] = jnp.zeros(asc.shape, F32)
    for p in range(nz):
        hit = ids_all == lax.rem(z + offs[p], nz) * NY + y
        asc[p : p + 1, :] = jnp.sum(jnp.where(hit, 1.0, 0.0), axis=0, keepdims=True)
        gsc[p : p + 1, :] = jnp.sum(jnp.where(hit, gates_all, 0.0), axis=0, keepdims=True)
    l0 = lax.broadcasted_iota(jnp.int32, (lanes, lanes), 0)
    l1 = lax.broadcasted_iota(jnp.int32, (lanes, lanes), 1)
    earlier = jnp.where((l0 // PAD == l1 // PAD) & (l0 < l1), 1.0, 0.0).astype(BF16)
    csc[...] = nn(asc[...].astype(BF16), earlier)
    r2 = lax.broadcasted_iota(jnp.int32, (group, lanes), 0)
    b2 = lax.broadcasted_iota(jnp.int32, (group, lanes), 1) // PAD
    block = jnp.where(r2 // CAP == b2, 1.0, 0.0)
    rank = lax.rem(r2, CAP).astype(F32)
    for p in range(nz):
        pick = jnp.where(csc[p : p + 1, :] == rank, block, 0.0) * asc[p : p + 1, :]
        sel[p * group : (p + 1) * group, :] = pick.astype(BF16)
        selg[p * group : (p + 1) * group, :] = pick * gsc[p : p + 1, :]

    z_order = range(1, nz)
    for k in (0, 1):
        for d in range(1, NY):
            got(tok.at[k, pl.ds(d * PAD, PAD)], ("tok", k, d), ydev(d))
        picked = nn(sel[...], tok[k])
        if k == 1:
            picked = picked * jnp.sum(selg[...], axis=1, keepdims=True)
        zs[k] = picked.astype(BF16)
        for p in z_order:
            q = neg(p)
            put(
                zs.at[k, pl.ds(p * group, group)],
                g.at[k, x_t, pl.ds(q * group, group)],
                ("z", k, p),
                ("z", k, q),
                zdev(p),
            )
        g[k, x_t, 0:group, :] = zs[k, 0:group, :]

    for copy in loads:
        copy.wait()

    def piece(k, j, t):
        return g.at[k, t, pl.ds(j * crow, crow)]

    def pass_own(k, j):
        for p in range(j * per, (j + 1) * per):
            if p:
                got(g.at[k, x_t, pl.ds(p * group, group)], ("z", k, p), zdev(p))
        own = piece(k, j, x_t)
        for dx in (1, 3, 2):
            put(own, own, ("g", k, j, NX - dx), ("g", k, j, NX - dx), xdev(dx))
        put(own, own, ("g", k, j, "o0"), ("g", k, j, "o0"), partner)

    def hand_over(k, j, dx):
        ref = piece(k, j, tab(dx))
        got(ref, ("g", k, j, dx), xdev(dx))
        put(ref, ref, ("g", k, j, "o%d" % dx), ("g", k, j, "o%d" % dx), partner)

    def pass_near(k, j):
        for dx in (3, 1):
            hand_over(k, j, dx)

    def pass_far(k, j):
        hand_over(k, j, 2)

    steps = [(k, j) for k in (0, 1) for j in range(chunks)]

    def step(s):
        for wait, pass_on in ((s, pass_own), (s - 3, pass_far), (s - 2, pass_near)):
            if 0 <= wait < len(steps):
                pass_on(*steps[wait])

    def wait_other(k):
        for dx in (0, 3, 1, 2):
            for j in range(chunks):
                got(piece(k, j, tab(dx, 1)), ("g", k, j, "o%d" % dx), partner)

    for s in range(chunks):
        step(s)
    pre[...] = nn(g[0, tab(0)], wgu[tab(0)])
    for s in range(chunks, chunks + 2):
        step(s)
    for dx in (3, 1):
        pre[...] += nn(g[0, tab(dx)], wgu[tab(dx)])
    for s in range(chunks + 2, 2 * chunks):
        step(s)
    pre[...] += nn(g[0, tab(2)], wgu[tab(2)])
    wait_other(0)
    for dx in (0, 3, 1, 2):
        pre[...] += nn(g[0, tab(dx, 1)], wgu[tab(dx, 1)])
    gate_pre, up_pre = pre[:, 0:hidden], pre[:, hidden : 2 * hidden]
    hact[...] = (gate_pre * jax.nn.sigmoid(gate_pre) * up_pre).astype(BF16)

    def span(h):
        return pl.ds(h * (rows // 2), rows // 2)

    def part(k, h, t):
        if k == 0:
            return nn(hact[span(h), :], dn[t])
        return nt(gug[span(h), :], wgu[t])

    def pair_send(k, h, dx):
        pps[k, dx, span(h), :] = part(k, h, tab(dx, 1)).astype(BF16)
        put(
            pps.at[k, dx, span(h)],
            ppr.at[k, dx, span(h)],
            ("pp", k, h, dx),
            ("pp", k, h, dx),
            partner,
        )

    def pair_sum(k, h, dx):
        mine = part(k, h, tab(dx))
        got(ppr.at[k, dx, span(h)], ("pp", k, h, dx), partner)
        chip[k, dx, span(h), :] = (mine + ppr[k, dx, span(h), :].astype(F32)).astype(BF16)
        if dx:
            put(
                chip.at[k, dx, span(h)],
                nbr.at[k, NX - dx, span(h)],
                ("n", k, h, NX - dx),
                ("n", k, h, NX - dx),
                xdev(dx),
            )

    def reduce_start(k, h):
        pair_send(k, h, 2)
        pair_send(k, h, 1)
        pair_sum(k, h, 2)
        pair_send(k, h, 3)
        pair_sum(k, h, 1)
        pair_send(k, h, 0)
        pair_sum(k, h, 3)
        pair_sum(k, h, 0)

    def reduce_end(k, h):
        total = chip[k, 0, span(h), :].astype(F32)
        for dx in (3, 1, 2):
            got(nbr.at[k, dx, span(h)], ("n", k, h, dx), xdev(dx))
            total = total + nbr[k, dx, span(h), :].astype(F32)
        fin[k, span(h), :] = total.astype(BF16)
        for p in range(h * (nz // 2), (h + 1) * (nz // 2)):
            if p == 0:
                continue
            q = neg(p)
            put(
                fin.at[k, pl.ds(p * group, group)],
                ret.at[k, pl.ds(q * group, group)],
                ("back", k, p),
                ("back", k, q),
                zdev(p),
            )
        if h == 0:
            ret[k, 0:group, :] = fin[k, 0:group, :]

    step(2 * chunks)
    reduce_start(0, 1)
    for s in range(2 * chunks + 1, 2 * chunks + 3):
        step(s)
    reduce_start(0, 0)

    agr[...] = nt(g[1, tab(0)], dn[tab(0)])
    for dx in (3, 1, 2):
        agr[...] += nt(g[1, tab(dx)], dn[tab(dx)])
    wait_other(1)
    for dx in (0, 3, 1, 2):
        agr[...] += nt(g[1, tab(dx, 1)], dn[tab(dx, 1)])
    gate_pre, up_pre = pre[:, 0:hidden], pre[:, hidden : 2 * hidden]
    sig = jax.nn.sigmoid(gate_pre)
    act_grad = agr[...]
    gug[:, 0:hidden] = (act_grad * up_pre * sig * (1.0 + gate_pre * (1.0 - sig))).astype(BF16)
    gug[:, hidden : 2 * hidden] = (act_grad * (gate_pre * sig)).astype(BF16)

    reduce_start(1, 1)
    reduce_end(0, 1)
    reduce_start(1, 0)
    reduce_end(0, 0)

    def weight_grad(t):
        dgr[:, t * width : (t + 1) * width] = tn(hact[...], g[1, t]).astype(BF16)

    for t in range(slots):
        weight_grad(t)
    dgr_copy = pltpu.make_async_copy(dgr, dgr_o, loc_sem.at[0])
    dgr_copy.start()

    def combine(k):
        for p in range(1, nz):
            got(ret.at[k, pl.ds(p * group, group)], ("back", k, p), zdev(p))
        if k == 0:
            coarse = selg[...].astype(BF16)
            fine = (selg[...] - coarse.astype(F32)).astype(BF16)
            summed = tn(coarse, ret[k]) + tn(fine, ret[k])
        else:
            summed = tn(sel[...], ret[k])
        ys[k] = summed.astype(BF16)
        for d in y_order:
            put(
                ys.at[k, pl.ds(d * PAD, PAD)],
                yr.at[k, NY - d],
                ("ys", k, d),
                ("ys", k, NY - d),
                ydev(d),
            )

    def finish(k, out):
        total = ys[k, 0:PAD, :].astype(F32)
        for d in range(1, NY):
            got(yr.at[k, d], ("ys", k, d), ydev(d))
            total = total + yr[k, d].astype(F32)
        out[...] = total[0:token_count, :].astype(BF16)

    reduce_end(1, 1)
    reduce_end(1, 0)
    combine(0)
    combine(1)
    finish(0, mix_o)
    finish(1, ing_o)

    dgr_copy.wait()
    for copy in sends:
        copy.wait_send()
    assert len(ssems.index) <= send_sem.shape[0] and len(rsems.index) <= recv_sem.shape[0]


def on_device(hidden_in, expert_ids, gate_weights, out_grad, gate_weight, up_weight, down_weight):
    token_count, per_token = expert_ids.shape
    nz = lax.axis_size("expert") // NY
    width = hidden_in.shape[1]
    hidden = gate_weight.shape[2]
    slots = NX * NC
    rows = nz * NY * CAP
    lanes = NY * PAD
    chunks = 4 if nz % 4 == 0 else 2
    copies = 2 * (NY - 1) * 3 + 4 * (nz - 1) + 2 * 7 * chunks + 96
    vmem = pl.BlockSpec(memory_space=pltpu.VMEM)
    hbm = pl.BlockSpec(memory_space=pltpu.HBM)
    mixed, input_grad, down_grad = pl.pallas_call(
        functools.partial(kernel, nz, chunks, (token_count, width, hidden)),
        out_shape=(
            jax.ShapeDtypeStruct((token_count, width), BF16),
            jax.ShapeDtypeStruct((token_count, width), BF16),
            jax.ShapeDtypeStruct((hidden, slots * width), BF16),
        ),
        in_specs=[hbm] * 7,
        out_specs=(vmem, vmem, hbm),
        scratch_shapes=[
            pltpu.VMEM((token_count, width), BF16),
            pltpu.VMEM((per_token, token_count), jnp.int32),
            pltpu.VMEM((per_token, token_count), F32),
            pltpu.VMEM((token_count, width), BF16),
            pltpu.VMEM((2, lanes, width), BF16),
            pltpu.VMEM((NY, per_token, lanes), F32),
            pltpu.VMEM((2, rows, width), BF16),
            pltpu.VMEM((2, slots, rows, width), BF16),
            pltpu.VMEM((slots, width, 2 * hidden), BF16),
            pltpu.VMEM((slots, hidden, width), BF16),
            pltpu.VMEM((16, lanes), F32),
            pltpu.VMEM((16, lanes), F32),
            pltpu.VMEM((16, lanes), F32),
            pltpu.VMEM((rows, lanes), BF16),
            pltpu.VMEM((rows, lanes), F32),
            pltpu.VMEM((rows, 2 * hidden), F32),
            pltpu.VMEM((rows, hidden), F32),
            pltpu.VMEM((rows, hidden), BF16),
            pltpu.VMEM((rows, 2 * hidden), BF16),
            pltpu.VMEM((hidden, slots * width), BF16),
            pltpu.VMEM((2, NX, rows, width), BF16),
            pltpu.VMEM((2, NX, rows, width), BF16),
            pltpu.VMEM((2, NX, rows, width), BF16),
            pltpu.VMEM((2, NX, rows, width), BF16),
            pltpu.VMEM((2, rows, width), BF16),
            pltpu.VMEM((2, rows, width), BF16),
            pltpu.VMEM((2, lanes, width), BF16),
            pltpu.VMEM((2, NY, PAD, width), BF16),
            pltpu.SemaphoreType.DMA((copies,)),
            pltpu.SemaphoreType.DMA((copies,)),
            pltpu.SemaphoreType.DMA((3 * slots + 4,)),
        ],
        compiler_params=pltpu.CompilerParams(
            collective_id=0, has_side_effects=True, vmem_limit_bytes=48 << 20
        ),
    )(
        *(
            pltpu.with_memory_space_constraint(a, pltpu.HBM)
            for a in (
                hidden_in,
                expert_ids.T,
                gate_weights.T,
                out_grad,
                gate_weight[0],
                up_weight[0],
                down_weight[0],
            )
        )
    )
    return mixed, input_grad, down_grad[None]


def solution(mesh):
    return jax.shard_map(
        on_device,
        mesh=mesh,
        in_specs=(
            P("expert", "etp"),
            P("expert", None),
            P("expert", None),
            P("expert", "etp"),
            P("expert", None, "etp"),
            P("expert", None, "etp"),
            P("expert", "etp", None),
        ),
        out_specs=(P("expert", "etp"), P("expert", "etp"), P("expert", "etp", None)),
        check_vma=False,
    )
```
